32 devices in a mesh: dp: 8 (over y, x, core), mp: 4 (over z).
Axes of the slice: x: 2, y: 2, z: 4, core: 2. Of those that a mesh axis runs over, the one named last changes fastest.
Arguments:
- hidden: bfloat16 [4096, 768], P('dp'), may hold values from -6 to 6
- memory: bfloat16 [32768, 768], P('dp', 'mp'), may hold values from -6 to 6
- out_grad: bfloat16 [4096, 768], P('dp'), may hold values from -6 to 6
- dec_starts: int32 [32, 4], P('dp'), may hold values from 0 to 127, as said below
- dec_length: int32 [32], P('dp'), may hold values from 96 to 128
- mem_starts: int32 [32, 4], P('dp'), may hold values from 0 to 1023, as said below
- mem_length: int32 [32], P('dp'), may hold values from 768 to 1024
- self_qkv: bfloat16 [3, 768, 768], P(None, None, 'mp'), may hold values from -0.25 to 0.25
- self_qv_bias: float32 [2, 768], P(None, 'mp'), may hold values from -3 to 3
- self_proj: bfloat16 [768, 768], P('mp'), may hold values from -0.3125 to 0.3125
- cross_query: bfloat16 [768, 768], P(None, 'mp'), may hold values from -0.25 to 0.25
- cross_kv: bfloat16 [2, 768, 768], P(None, None, 'mp'), may hold values from -0.25 to 0.25
- cross_qv_bias: float32 [2, 768], P(None, 'mp'), may hold values from -3 to 3
- cross_proj: bfloat16 [768, 768], P('mp'), may hold values from -0.875 to 0.875
- ffn_in: bfloat16 [768, 3072], P(None, 'mp'), may hold values from -0.21875 to 0.21875
- ffn_in_bias: float32 [3072], P('mp'), may hold values from -3 to 3
- ffn_out: bfloat16 [3072, 768], P('mp'), may hold values from -0.15625 to 0.15625
- out_biases: float32 [3, 768], replicated, may hold values from -3 to 3
- norm_gains: float32 [3, 768], replicated, may hold values from 0.25 to 1.75
- norm_biases: float32 [3, 768], replicated, may hold values from -2 to 2
Outputs:
- result: bfloat16 [4096, 768], P('dp')
- hidden_grad: float32 [4096, 768], P('dp')
- memory_grad: float32 [32768, 768], P('dp', 'mp')
- self_qkv_grad: float32 [3, 768, 768], P(None, None, 'mp')
- self_qv_bias_grad: float32 [2, 768], P(None, 'mp')
- self_proj_grad: float32 [768, 768], P('mp')
- cross_query_grad: float32 [768, 768], P(None, 'mp')
- cross_kv_grad: float32 [2, 768, 768], P(None, None, 'mp')
- cross_qv_bias_grad: float32 [2, 768], P(None, 'mp')
- cross_proj_grad: float32 [768, 768], P('mp')
- ffn_in_grad: float32 [768, 3072], P(None, 'mp')
- ffn_in_bias_grad: float32 [3072], P('mp')
- ffn_out_grad: float32 [3072, 768], P('mp')
- out_biases_grad: float32 [3, 768], replicated
- norm_gains_grad: float32 [3, 768], replicated
- norm_biases_grad: float32 [3, 768], replicated
The draws below stay inside these ranges and needn't reach their ends.
Inputs may be any that keep to these rules, and one draw needn't show every extreme that they name: `dec_starts`: each packed row holds 4 pairs; its offsets start at 0, rise strictly and stay below the row's used slots, so every decoder segment holds at least one used slot; padded slots belong to the last pair. `mem_starts`: pair j's table is memory segment j of the same packed row; offsets start at 0, rise strictly and stay below the row's used slots, so every memory segment holds at least one used slot.
All inputs are finite; a program needn't handle non-finite values.
Results may differ from the reference program's by a relative error of at most 0.023.
Values may be sent and summed in bfloat16 or wider, within the bound.
No kernel may reach another device: no remote copies, remote signals or barrier semaphores. Data moves between devices by JAX's collectives and lax.ppermute only.
A program may use at most 128 MiB of HBM per device.

```python
import math
import jax
import jax.numpy as jnp
from jax import lax

D = 768
HEADS = 12
HD = 64
FF = 3072
LQ = 128
LM = 1024
NSEG = 4
ROWS = 32
TOKENS = 4096
MEM_TOKENS = 32768


def layout(key, slot_count):
    pad_key, pick_key, share_key = jax.random.split(key, 3)
    most_pad = slot_count // 4
    padding = jax.random.randint(pad_key, (ROWS,), 0, most_pad + 1)
    ordering = jax.random.permutation(pick_key, ROWS)
    padding = padding.at[ordering[0]].set(0).at[ordering[1]].set(most_pad)
    lengths = slot_count - padding
    shares = jax.random.randint(share_key, (ROWS, NSEG), 1, 4)
    before = jnp.cumsum(shares, axis=1) - shares
    totals = jnp.sum(shares, axis=1)
    starts = lengths[:, None] * before // totals[:, None]
    starts = starts.at[ordering[0], NSEG - 1].set(slot_count - 1)
    return (starts.astype(jnp.int32), lengths.astype(jnp.int32))


def draw_dec_starts(key, part):
    return layout(jax.random.fold_in(key, 11), LQ)[0]


def draw_dec_length(key, part):
    return layout(jax.random.fold_in(key, 11), LQ)[1]


def draw_mem_starts(key, part):
    return layout(jax.random.fold_in(key, 23), LM)[0]


def draw_mem_length(key, part):
    return layout(jax.random.fold_in(key, 23), LM)[1]


def block_scale(own_key, shape, cuts, low, largest):
    gain = 1.0
    for axis_at, parts in cuts:
        heights = jax.random.uniform(jax.random.fold_in(jax.random.fold_in(own_key, 6), axis_at), (parts,), jnp.float32, low / len(cuts), largest / len(cuts))
        gain = gain * jnp.repeat(jnp.exp(heights), shape[axis_at] // parts).reshape((-1,) + (1,) * (len(shape) - 1 - axis_at))
    return gain


def scatter_about(rng, dims, spread, bound, cuts=(), kind=jnp.bfloat16):
    factor_of = block_scale(rng, dims, cuts, -0.22, 0.18) if cuts else 1.0
    result = jax.random.normal(rng, dims, jnp.float32) * spread * factor_of
    return jnp.minimum(jnp.maximum(result, -bound), bound).astype(kind)


def setup_inputs(seed: int = 0) -> dict:
    seeds = jax.random.split(jax.random.key(seed), 21)
    hidden = scatter_about(seeds[0], (TOKENS, D), 1.0, 6.0, ((0, 8),))
    memory = scatter_about(seeds[1], (MEM_TOKENS, D), 1.0, 6.0, ((0, 8), (1, 4)))
    out_grad = scatter_about(seeds[2], (TOKENS, D), 1.0, 6.0, ((0, 8),))
    dec_starts = draw_dec_starts(jax.random.fold_in(seeds[20], 71), 0)
    dec_length = draw_dec_length(jax.random.fold_in(seeds[20], 71), 0)
    mem_starts = draw_mem_starts(jax.random.fold_in(seeds[20], 71), 0)
    mem_length = draw_mem_length(jax.random.fold_in(seeds[20], 71), 0)
    self_qkv = scatter_about(seeds[7], (3, D, D), (2 * D // 3) ** -0.5, 0.25, ((2, 4),))
    self_qv_bias = scatter_about(seeds[8], (2, D), 0.5, 3.0, ((1, 4),), jnp.float32)
    self_proj = scatter_about(seeds[9], (D, D), (D // 2) ** -0.5, 0.3125, ((0, 4),))
    cross_query = scatter_about(seeds[10], (D, D), (2 * D // 3) ** -0.5, 0.25, ((1, 4),))
    cross_kv = scatter_about(seeds[11], (2, D, D), (2 * D // 3) ** -0.5, 0.25, ((2, 4),))
    cross_qv_bias = scatter_about(seeds[12], (2, D), 0.5, 3.0, ((1, 4),), jnp.float32)
    cross_proj = scatter_about(seeds[13], (D, D), (D // 16) ** -0.5, 0.875, ((0, 4),))
    ffn_in = scatter_about(seeds[14], (D, FF), D ** -0.5, 0.21875, ((1, 4),))
    ffn_in_bias = scatter_about(seeds[15], (FF,), 0.5, 3.0, ((0, 4),), jnp.float32)
    ffn_out = scatter_about(seeds[16], (FF, D), (FF // 2) ** -0.5, 0.15625, ((0, 4),))
    out_biases = scatter_about(seeds[17], (3, D), 0.5, 3.0, (), jnp.float32)
    norm_gains = jnp.clip(1.0 + 0.15 * jax.random.normal(seeds[18], (3, D), jnp.float32), 0.25, 1.75)
    norm_biases = scatter_about(seeds[19], (3, D), 0.3, 2.0, (), jnp.float32)
    return dict(hidden=hidden, memory=memory, out_grad=out_grad, dec_starts=dec_starts, dec_length=dec_length, mem_starts=mem_starts, mem_length=mem_length, self_qkv=self_qkv, self_qv_bias=self_qv_bias, self_proj=self_proj, cross_query=cross_query, cross_kv=cross_kv, cross_qv_bias=cross_qv_bias, cross_proj=cross_proj, ffn_in=ffn_in, ffn_in_bias=ffn_in_bias, ffn_out=ffn_out, out_biases=out_biases, norm_gains=norm_gains, norm_biases=norm_biases)


@jax.custom_vjp
def low(v):
    return lax.optimization_barrier(v.astype(jnp.bfloat16)).astype(jnp.float32)

@jax.custom_vjp
def low_back(v):
    return v

def low_keep(v):
    return (low(v), None)

def low_pass(kept, grad):
    return (grad,)

def back_keep(v):
    return (v, None)

def back_low(kept, grad):
    return (low(grad),)
low.defvjp(low_keep, low_pass)
low_back.defvjp(back_keep, back_low)
NEG_FILL = -1000000000.0
EPSILON = 1e-05
HIGHEST_PRECISION = lax.Precision.HIGHEST

def matmul(left_side, right_side):
    return jnp.dot(left_side, right_side, precision=HIGHEST_PRECISION, preferred_element_type=jnp.float32)

def layer_norm(values, gain_row, bias_row):
    average = lax.optimization_barrier(jnp.mean(values, -1, keepdims=True))
    centered = values - average
    variance = lax.optimization_barrier(jnp.mean(centered * centered, -1, keepdims=True))
    return centered * lax.rsqrt(variance + EPSILON) * gain_row + bias_row

def segment_ids(starts, slot_count):
    places = jnp.arange(slot_count, dtype=jnp.int32)
    return lax.optimization_barrier(jnp.sum((starts[:, None, :] <= places[None, :, None]).astype(jnp.int32), -1)) - 1

def attention(queries, key_rows, value_rows, allowed):
    row_count = allowed.shape[0]
    heads_q = queries.reshape(row_count, allowed.shape[1], HEADS, HD)
    heads_k = key_rows.reshape(row_count, allowed.shape[2], HEADS, HD)
    heads_v = value_rows.reshape(row_count, allowed.shape[2], HEADS, HD)
    scores = low_back(jnp.einsum('rqhd,rkhd->rhqk', heads_q, heads_k, precision=HIGHEST_PRECISION))
    scores = jnp.where(allowed[:, None], scores, NEG_FILL)
    prob_low = low(jax.nn.softmax(scores, axis=-1))
    output = jnp.einsum('rhqk,rkhd->rqhd', prob_low, heads_v, precision=HIGHEST_PRECISION)
    return output.reshape(row_count * allowed.shape[1], HEADS * HD)

def forward(hidden_rows, memory_rows, params, self_allowed, cross_allowed):
    self_qkv, self_qv_bias, self_proj, cross_query, cross_kv, cross_qv_bias, cross_proj, ffn_in, ffn_in_bias, ffn_out, out_biases, norm_gains, norm_biases = params
    scaling = HD ** (-0.5)
    self_q = (low_back(matmul(hidden_rows, self_qkv[0])) + self_qv_bias[0]) * scaling
    self_k = low_back(matmul(hidden_rows, self_qkv[1]))
    self_v = low_back(matmul(hidden_rows, self_qkv[2])) + self_qv_bias[1]
    self_o = low(low_back(attention(low(self_q), low(self_k), low(self_v), self_allowed)))
    first = layer_norm(hidden_rows + low_back(matmul(self_o, self_proj)) + out_biases[0], norm_gains[0], norm_biases[0])
    first_low = low(first)
    cross_q = (low_back(matmul(first_low, cross_query)) + cross_qv_bias[0]) * scaling
    cross_k = low_back(matmul(memory_rows, cross_kv[0]))
    cross_v = low_back(matmul(memory_rows, cross_kv[1])) + cross_qv_bias[1]
    cross_o = low(low_back(attention(low(cross_q), low(cross_k), low(cross_v), cross_allowed)))
    second = layer_norm(first + low_back(matmul(cross_o, cross_proj)) + out_biases[1], norm_gains[1], norm_biases[1])
    second_low = low(second)
    hidden_pre = low_back(matmul(second_low, ffn_in)) + ffn_in_bias
    activated = low(jax.nn.gelu(hidden_pre, approximate=False))
    return layer_norm(second + low_back(matmul(activated, ffn_out)) + out_biases[2], norm_gains[2], norm_biases[2])

def reference(hidden, memory, out_grad, dec_starts, dec_length, mem_starts, mem_length, self_qkv, self_qv_bias, self_proj, cross_query, cross_kv, cross_qv_bias, cross_proj, ffn_in, ffn_in_bias, ffn_out, out_biases, norm_gains, norm_biases):
    row_total = dec_starts.shape[0]
    group_rows = math.gcd(row_total, 8)
    step_count = row_total // group_rows
    params = tuple((member.astype(jnp.float32) for member in (self_qkv, self_qv_bias, self_proj, cross_query, cross_kv, cross_qv_bias, cross_proj, ffn_in, ffn_in_bias, ffn_out, out_biases, norm_gains, norm_biases)))
    dec_places = jnp.arange(LQ, dtype=jnp.int32)
    mem_places = jnp.arange(LM, dtype=jnp.int32)

    def scan_step(running, pieces):
        hidden_rows, memory_rows, grad_rows, dec_first, dec_used, mem_first, mem_used = pieces
        dec_segment = segment_ids(dec_first, LQ)
        mem_segment = segment_ids(mem_first, LM)
        self_allowed = (dec_segment[:, :, None] == dec_segment[:, None, :]) & (dec_places[None, None, :] <= dec_places[None, :, None]) & (dec_places[None, None, :] < dec_used[:, None, None])
        cross_allowed = (dec_segment[:, :, None] == mem_segment[:, None, :]) & (mem_places[None, None, :] < mem_used[:, None, None])

        def group_forward(hidden_part, memory_part, weights):
            return forward(hidden_part, memory_part, weights, self_allowed, cross_allowed)
        output, pullback = jax.vjp(group_forward, hidden_rows.astype(jnp.float32), memory_rows.astype(jnp.float32), params)
        hidden_grad, memory_grad, weight_grads = pullback(grad_rows.astype(jnp.float32))
        running = jax.tree.map(lambda left_side, right_side: left_side + right_side, running, weight_grads)
        return (running, (output.astype(jnp.bfloat16), hidden_grad, memory_grad))
    initial = jax.tree.map(jnp.zeros_like, params)
    pieces = (hidden.reshape(step_count, group_rows * LQ, D), memory.reshape(step_count, group_rows * LM, D), out_grad.reshape(step_count, group_rows * LQ, D), dec_starts.reshape(step_count, group_rows, NSEG), dec_length.reshape(step_count, group_rows), mem_starts.reshape(step_count, group_rows, NSEG), mem_length.reshape(step_count, group_rows))
    totals, (outputs, hidden_grads, memory_grads) = lax.scan(scan_step, initial, pieces)
    self_qkv_grad, self_qv_bias_grad, self_proj_grad, cross_query_grad, cross_kv_grad, cross_qv_bias_grad, cross_proj_grad, ffn_in_grad, ffn_in_bias_grad, ffn_out_grad, out_biases_grad, norm_gains_grad, norm_biases_grad = totals
    return (outputs.reshape(row_total * LQ, D), hidden_grads.reshape(row_total * LQ, D), memory_grads.reshape(row_total * LM, D), self_qkv_grad, self_qv_bias_grad, self_proj_grad, cross_query_grad, cross_kv_grad, cross_qv_bias_grad, cross_proj_grad, ffn_in_grad, ffn_in_bias_grad, ffn_out_grad, out_biases_grad, norm_gains_grad, norm_biases_grad)
```

```python
import jax
import jax.numpy as jnp
from jax import lax
from jax.experimental import pallas as pl
from jax.experimental.pallas import tpu as pltpu
from jax.sharding import PartitionSpec as P

HD = 64
NEG_FILL = -1000000000.0
EPSILON = 1e-05
BF = jnp.bfloat16
F32 = jnp.float32


def segment_ids(starts, slot_count):
    places = jnp.arange(slot_count, dtype=jnp.int32)
    return jnp.sum((starts[:, None, :] <= places[None, :, None]).astype(jnp.int32), -1) - 1


def layer_norm(values, gain_row, bias_row):
    average = jnp.mean(values, -1, keepdims=True)
    centered = values - average
    variance = jnp.mean(centered * centered, -1, keepdims=True)
    return centered * lax.rsqrt(variance + EPSILON) * gain_row + bias_row


def exact_gelu(values):
    return jax.nn.gelu(values, approximate=False)


def mm(left_side, right_side, dims):
    return lax.dot_general(left_side, right_side, (dims, ((), ())), preferred_element_type=F32)


def inner_dot(left_side, right_side):
    return mm(left_side, right_side, ((0,), (0,)))


def outer_dot(left_side, right_side):
    return mm(left_side, right_side, ((1,), (1,)))


def plain_dot(left_side, right_side):
    return mm(left_side, right_side, ((1,), (0,)))


def attend_block(queries, key_rows, value_rows, allowed):
    scores = jnp.einsum("rqhd,rkhd->rhqk", queries, key_rows, preferred_element_type=F32)
    scores = jnp.where(allowed[:, None], scores, NEG_FILL)
    peak_score = jnp.max(scores, -1, keepdims=True)
    weights = jnp.exp(scores - peak_score)
    totals = jnp.sum(weights, -1, keepdims=True)
    prob_low = (weights / totals).astype(BF)
    output = jnp.einsum("rhqk,rkhd->rqhd", prob_low, value_rows, preferred_element_type=F32)
    return (output, (peak_score + jnp.log(totals))[..., 0])


def attend_back(queries, key_rows, value_rows, allowed, log_total, grad_rows):
    scores = jnp.einsum("rqhd,rkhd->rhqk", queries, key_rows, preferred_element_type=F32)
    scores = jnp.where(allowed[:, None], scores, NEG_FILL)
    prob_full = jnp.exp(scores - log_total[..., None])
    prob_low = prob_full.astype(BF)
    value_grad = jnp.einsum("rhqk,rqhd->rkhd", prob_low, grad_rows, preferred_element_type=F32)
    prob_grad = jnp.einsum("rqhd,rkhd->rhqk", grad_rows, value_rows, preferred_element_type=F32)
    offset = jnp.sum(prob_full * prob_grad, -1, keepdims=True)
    score_grad = (prob_full * (prob_grad - offset)).astype(BF)
    query_grad = jnp.einsum("rhqk,rkhd->rqhd", score_grad, key_rows, preferred_element_type=F32)
    key_grad = jnp.einsum("rhqk,rqhd->rkhd", score_grad, queries, preferred_element_type=F32)
    return (query_grad, key_grad, value_grad)


def shuffle_kernel(index_ref, source_ref, target_ref):
    for place in range(target_ref.shape[0]):
        target_ref[place] = source_ref[index_ref[place]]


def shuffle(source, index):
    return pl.pallas_call(
        shuffle_kernel,
        out_shape=jax.ShapeDtypeStruct((index.shape[0],) + source.shape[1:], source.dtype),
        in_specs=[
            pl.BlockSpec(memory_space=pltpu.SMEM),
            pl.BlockSpec(memory_space=pltpu.VMEM),
        ],
        out_specs=pl.BlockSpec(memory_space=pltpu.VMEM),
        cost_estimate=pl.CostEstimate(
            flops=0, transcendentals=0, bytes_accessed=4 * source.size
        ),
    )(index, source)


def pick(stacked, place):
    return lax.dynamic_index_in_dim(stacked, place, 0, keepdims=False)


def after(value, *others):
    return lax.optimization_barrier((value,) + others)[0]


class Links:
    def __init__(self, dp_size, mp_size):
        self.dp_size, self.mp_size = dp_size, mp_size
        self.dp_bits = dp_size.bit_length() - 1
        rest = list(range(1, self.dp_bits))
        self.orders = ([0] + rest, [0] + rest[::-1])
        self.dp_at = lax.axis_index("dp")
        self.mp_at = lax.axis_index("mp")

    def swap_dp(self, value, bit):
        return lax.ppermute(value, "dp", [(i, i ^ (1 << bit)) for i in range(self.dp_size)])

    def swap_mp(self, value, step):
        return lax.ppermute(value, "mp", [(i, i ^ step) for i in range(self.mp_size)])

    def exchange_mp(self, blocks):
        return [pick(blocks, self.mp_at)] + [
            self.swap_mp(pick(blocks, self.mp_at ^ step), step)
            for step in range(1, self.mp_size)
        ]

    def spread_mp(self, value):
        return [value] + [self.swap_mp(value, step) for step in range(1, self.mp_size)]

    def ordered_mp(self, pieces):
        stacked = jnp.stack(pieces)
        return [pick(stacked, self.mp_at ^ place) for place in range(self.mp_size)]

    def reduce_mp(self, blocks):
        pieces = self.exchange_mp(blocks)
        total = pieces[0].astype(F32)
        for piece in pieces[1:]:
            total = total + piece.astype(F32)
        return total

    def scatter_dp(self, value, order):
        current = value.reshape((2,) * self.dp_bits + value.shape[1:])
        axes = list(range(self.dp_bits))[::-1]
        for bit in order:
            axis = axes.index(bit)
            mine = (self.dp_at >> bit) & 1
            kept = lax.dynamic_index_in_dim(current, mine, axis, keepdims=False)
            sent = lax.dynamic_index_in_dim(current, 1 - mine, axis, keepdims=False)
            received = self.swap_dp(sent.astype(BF), bit)
            current = kept.astype(F32) + received.astype(F32)
            axes.pop(axis)
            if axes:
                current = current.astype(BF)
        return current

    def gather_dp(self, value, order):
        current = value[None]
        bits = []
        for bit in order[::-1]:
            current = jnp.concatenate([current, self.swap_dp(current, bit)], 0)
            bits = [bit] + bits
        return current, bits

    def flat_place(self, member, bits):
        apart = member ^ self.dp_at
        place = 0
        for position, bit in enumerate(bits[::-1]):
            place = place + (((apart >> bit) & 1) << position)
        return place

    def gather_weight(self, rows, order):
        gathered, bits = self.gather_dp(rows, order)
        flat = gathered.reshape((-1,) + rows.shape[1:])
        members = jnp.arange(self.dp_size, dtype=jnp.int32)
        dp_place = self.flat_place(members, bits)
        mp_place = jnp.arange(self.mp_size, dtype=jnp.int32) ^ self.mp_at
        index = dp_place[None, :] * self.mp_size + mp_place[:, None]
        return shuffle(flat, index.reshape(-1).astype(jnp.int32))

    def gather_grad(self, slab, order):
        gathered, bits = self.gather_dp(slab, order)
        members = jnp.arange(self.dp_size, dtype=jnp.int32)
        return shuffle(gathered, self.flat_place(members, bits).astype(jnp.int32))


def pack_tokens(values):
    half = values.shape[0] // 2
    return jnp.concatenate([values[:half], values[half:]], axis=1)


def unpack_tokens(values):
    half = values.shape[1] // 2
    return jnp.concatenate([values[:, :half], values[:, half:]], axis=0)


def body(
    dp_size,
    mp_size,
    hidden,
    memory,
    out_grad,
    dec_starts,
    dec_length,
    mem_starts,
    mem_length,
    self_qkv,
    self_qv_bias,
    self_proj,
    cross_query,
    cross_kv,
    cross_qv_bias,
    cross_proj,
    ffn_in,
    ffn_in_bias,
    ffn_out,
    out_biases,
    norm_gains,
    norm_biases,
):
    net = Links(dp_size, mp_size)
    order_a, order_b = net.orders
    row_count = dec_starts.shape[0]
    dec_slots = hidden.shape[0] // row_count
    mem_slots = memory.shape[0] // row_count
    width = hidden.shape[1]
    local_width = self_qkv.shape[2]
    local_ff = ffn_in.shape[1]
    head_count = local_width // HD
    all_heads = width // HD
    own_rows = row_count // mp_size
    own_tokens = own_rows * dec_slots
    own_memory = own_rows * mem_slots
    scaling = HD ** (-0.5)

    memory_blocks = jax.vmap(pack_tokens)(memory.reshape(mp_size, own_memory, local_width))
    memory_pieces = net.exchange_mp(memory_blocks)
    small = jnp.concatenate(
        [cross_qv_bias.reshape(-1), ffn_in_bias]
    ).reshape(-1, 128)
    small_all = jnp.stack(net.ordered_mp(net.spread_mp(small))).reshape(mp_size, -1)
    bias_all = small_all[:, : 2 * local_width].reshape(mp_size, 2, local_width)
    cross_q_bias = bias_all[:, 0].reshape(width)
    cross_v_bias = bias_all[:, 1].reshape(width)
    ffn_bias_all = small_all[:, 2 * local_width :].reshape(-1)

    def own_piece(rows):
        count = rows.shape[0] // dp_size
        return lax.dynamic_slice_in_dim(rows, net.dp_at * count, count, 0)

    def weights(first_rows, second_rows, hold=None):
        a_piece, b_piece = own_piece(first_rows), own_piece(second_rows)
        piece = jnp.concatenate([a_piece, b_piece], 0)
        if hold is not None:
            piece = after(piece, hold)
        both = jnp.stack(net.spread_mp(piece))
        count = a_piece.shape[0]
        whole_a = net.gather_weight(both[:, :count], order_a)
        whole_b = net.gather_weight(both[:, count:], order_b)
        return (
            whole_a.reshape((mp_size,) + first_rows.shape),
            whole_b.reshape((mp_size,) + second_rows.shape),
        )

    kv_rows = jnp.swapaxes(cross_kv, 1, 2).reshape(2 * local_width, width)
    qo_rows = jnp.concatenate([cross_query.T, cross_proj], 0)
    kv_all, qo_all = weights(kv_rows, qo_rows)
    kv_whole = jnp.swapaxes(
        kv_all.reshape(mp_size, 2, local_width, width), 0, 1
    ).reshape(2 * width, width)
    query_whole = qo_all[:, :local_width].reshape(width, width)
    proj_whole = qo_all[:, local_width:].reshape(width, width)

    dec_places = jnp.arange(dec_slots, dtype=jnp.int32)
    mem_places = jnp.arange(mem_slots, dtype=jnp.int32)
    dec_segment = segment_ids(dec_starts, dec_slots)
    self_allowed = (
        (dec_segment[:, :, None] == dec_segment[:, None, :])
        & (dec_places[None, None, :] <= dec_places[None, :, None])
        & (dec_places[None, None, :] < dec_length[:, None, None])
    )

    def own_of(values):
        return lax.dynamic_slice_in_dim(values, net.mp_at * own_rows, own_rows, 0)

    mem_segment = segment_ids(own_of(mem_starts), mem_slots)
    cross_allowed = (own_of(dec_segment)[:, :, None] == mem_segment[:, None, :]) & (
        mem_places[None, None, :] < own_of(mem_length)[:, None, None]
    )

    def split_heads(values, rows):
        return values.reshape(rows, values.shape[0] // rows, values.shape[1] // HD, HD)

    def merge_heads(values):
        return values.reshape(values.shape[0] * values.shape[1], -1)

    self_weight = jnp.concatenate([self_qkv[0], self_qkv[1], self_qkv[2]], axis=1)
    projected = plain_dot(hidden, self_weight)
    self_q = split_heads(
        ((projected[:, :local_width] + self_qv_bias[0]) * scaling).astype(BF), row_count
    )
    self_k = split_heads(projected[:, local_width : 2 * local_width].astype(BF), row_count)
    self_v = split_heads(
        (projected[:, 2 * local_width :] + self_qv_bias[1]).astype(BF), row_count
    )
    self_out, self_total = attend_block(self_q, self_k, self_v, self_allowed)
    self_low = merge_heads(self_out).astype(BF)
    self_part = plain_dot(self_low, self_proj).astype(BF)
    self_branch = net.reduce_mp(self_part.reshape(mp_size, own_tokens, width))

    hidden_own = pick(hidden.reshape(mp_size, own_tokens, width), net.mp_at)
    grad_own = pick(out_grad.reshape(mp_size, own_tokens, width), net.mp_at)
    first, first_back = jax.vjp(
        layer_norm,
        hidden_own.astype(F32) + self_branch + out_biases[0],
        norm_gains[0],
        norm_biases[0],
    )
    first_low = first.astype(BF)

    memory_own = jnp.concatenate(
        [unpack_tokens(piece) for piece in net.ordered_mp(memory_pieces)], axis=1
    )
    memory_kv = outer_dot(memory_own, kv_whole)
    cross_k = split_heads(memory_kv[:, :width].astype(BF), own_rows)
    cross_v = split_heads((memory_kv[:, width:] + cross_v_bias).astype(BF), own_rows)
    cross_pre = outer_dot(first_low, query_whole)
    cross_q = split_heads(((cross_pre + cross_q_bias) * scaling).astype(BF), own_rows)
    cross_out, cross_total = attend_block(cross_q, cross_k, cross_v, cross_allowed)
    cross_low = merge_heads(cross_out).astype(BF)
    ffn_in_all, ffn_out_all = weights(ffn_in, ffn_out, memory_own)
    second, second_back = jax.vjp(
        layer_norm,
        first + plain_dot(cross_low, proj_whole) + out_biases[1],
        norm_gains[1],
        norm_biases[1],
    )
    second_low = second.astype(BF)

    hidden_pre = jnp.concatenate(
        [plain_dot(second_low, ffn_in_all[place]) for place in range(mp_size)], 1
    )
    activated, gelu_back = jax.vjp(exact_gelu, hidden_pre + ffn_bias_all)
    activated_low = activated.astype(BF)
    ffn_out_whole = ffn_out_all.reshape(-1, width)
    final_norm, third_back = jax.vjp(
        layer_norm,
        second + plain_dot(activated_low, ffn_out_whole) + out_biases[2],
        norm_gains[2],
        norm_biases[2],
    )
    result = jnp.stack(net.ordered_mp(net.spread_mp(final_norm.astype(BF))))

    def shares(value):
        count = value.shape[1] // dp_size
        return jnp.swapaxes(value.reshape(mp_size, dp_size, count, width), 0, 1)

    def reduce_pair(first_value, second_value):
        a_slab = net.scatter_dp(shares(first_value), order_a)
        b_slab = net.scatter_dp(shares(second_value), order_b)
        count = a_slab.shape[1]
        both = net.reduce_mp(jnp.concatenate([a_slab, b_slab], 1).astype(BF)).astype(BF)
        a_whole = net.gather_grad(both[:count], order_a).reshape(-1, width)
        b_whole = net.gather_grad(both[count:], order_b).reshape(-1, width)
        return a_whole, b_whole

    third_grad, gain_three, shift_three = third_back(grad_own.astype(F32))
    third_low = third_grad.astype(BF)
    ffn_bias_out = jnp.sum(third_grad, 0)
    (pre_grad,) = gelu_back(outer_dot(third_low, ffn_out_whole))
    ffn_bias_in = jnp.sum(pre_grad, 0)
    pre_low = pre_grad.astype(BF)
    second_grad = third_grad
    for place in range(mp_size):
        second_grad = second_grad + outer_dot(
            pre_low[:, place * local_ff : (place + 1) * local_ff], ffn_in_all[place]
        )
    ffn_in_part = jnp.stack(
        [
            inner_dot(second_low, pre_low[:, place * local_ff : (place + 1) * local_ff]).astype(BF)
            for place in range(mp_size)
        ]
    )
    ffn_out_part = inner_dot(activated_low, third_low).astype(BF)
    ffn_in_grad, ffn_out_grad = reduce_pair(
        ffn_in_part, ffn_out_part.reshape(mp_size, local_ff, width)
    )

    cross_grad, gain_two, shift_two = second_back(second_grad)
    cross_grad_low = cross_grad.astype(BF)
    cross_bias_out = jnp.sum(cross_grad, 0)
    proj_part = inner_dot(cross_low, cross_grad_low).astype(BF)
    cross_out_grad = split_heads(outer_dot(cross_grad_low, proj_whole).astype(BF), own_rows)
    cq_grad, ck_grad, cv_grad = attend_back(
        cross_q, cross_k, cross_v, cross_allowed, cross_total, cross_out_grad
    )
    cq_grad = merge_heads(cq_grad) * scaling
    cv_grad = merge_heads(cv_grad)
    cross_q_sum, cross_v_sum = jnp.sum(cq_grad, 0), jnp.sum(cv_grad, 0)
    cq_low = cq_grad.astype(BF)
    first_grad = cross_grad + plain_dot(cq_low, query_whole)
    kv_low = jnp.concatenate([merge_heads(ck_grad), cv_grad], axis=1).astype(BF)
    memory_part = plain_dot(kv_low, kv_whole).astype(BF)
    memory_parts = jnp.stack(
        [
            pack_tokens(memory_part[:, place * local_width : (place + 1) * local_width])
            for place in range(mp_size)
        ]
    )
    memory_rows = net.ordered_mp(net.exchange_mp(memory_parts))
    memory_grad = jnp.concatenate([unpack_tokens(piece) for piece in memory_rows], 0).astype(F32)

    self_grad, gain_one, shift_one = first_back(first_grad)
    self_grad_low = self_grad.astype(BF)
    self_bias_out = jnp.sum(self_grad, 0)
    self_grad_all = jnp.concatenate(net.ordered_mp(net.spread_mp(self_grad_low)), 0)

    query_part = inner_dot(cq_low, first_low).astype(BF)
    kv_part = inner_dot(kv_low, memory_own).astype(BF)
    kv_share = jnp.swapaxes(
        kv_part.reshape(2, mp_size, local_width, width), 0, 1
    ).reshape(mp_size, 2 * local_width, width)
    qo_share = jnp.concatenate(
        [
            query_part.reshape(mp_size, local_width, width),
            proj_part.reshape(mp_size, local_width, width),
        ],
        1,
    )
    kv_grad, qo_grad = reduce_pair(kv_share, qo_share)
    cross_kv_grad = jnp.swapaxes(
        kv_grad.astype(F32).reshape(2, local_width, width), 1, 2
    )
    cross_query_grad = qo_grad[:local_width].astype(F32).T
    cross_proj_grad = qo_grad[local_width:].astype(F32)

    self_out_grad = split_heads(outer_dot(self_grad_all, self_proj).astype(BF), row_count)
    sq_grad, sk_grad, sv_grad = attend_back(
        self_q, self_k, self_v, self_allowed, self_total, self_out_grad
    )
    sq_grad = merge_heads(sq_grad) * scaling
    sv_grad = merge_heads(sv_grad)
    self_qv_sum = jnp.stack([jnp.sum(sq_grad, 0), jnp.sum(sv_grad, 0)])
    qkv_low = jnp.concatenate([sq_grad, merge_heads(sk_grad), sv_grad], axis=1).astype(BF)
    hidden_part = outer_dot(qkv_low, self_weight).astype(BF)
    hidden_sum = self_grad + net.reduce_mp(hidden_part.reshape(mp_size, own_tokens, width))
    hidden_grad = jnp.concatenate(
        net.ordered_mp(net.spread_mp(hidden_sum.astype(BF))), 0
    ).astype(F32)
    qkv_part = inner_dot(qkv_low, hidden).astype(BF)
    so_part = inner_dot(self_low, self_grad_all).astype(BF)

    def self_shares(value):
        return value.reshape(dp_size, -1, width)

    self_a = net.scatter_dp(self_shares(qkv_part[: 2 * local_width]), order_a)
    self_b = net.scatter_dp(
        self_shares(jnp.concatenate([qkv_part[2 * local_width :], so_part], 0)), order_b
    )
    self_a = net.gather_grad(self_a.astype(BF), order_a).reshape(-1, width).astype(F32)
    self_b = net.gather_grad(self_b.astype(BF), order_b).reshape(-1, width).astype(F32)
    self_qkv_grad = jnp.swapaxes(
        jnp.stack([self_a[:local_width], self_a[local_width:], self_b[:local_width]]), 1, 2
    )
    self_proj_grad = self_b[local_width:]

    self_qv_wide = lax.dynamic_update_slice_in_dim(
        jnp.zeros((2, width), F32), self_qv_sum, net.mp_at * local_width, 1
    )
    smalls = jnp.concatenate(
        [
            jnp.stack([self_bias_out, cross_bias_out, ffn_bias_out]),
            jnp.stack([gain_one, gain_two, gain_three]),
            jnp.stack([shift_one, shift_two, shift_three]),
            cross_q_sum[None],
            cross_v_sum[None],
            self_qv_wide,
            ffn_bias_in.reshape(-1, width),
        ],
        0,
    )
    for bit in range(net.dp_bits):
        smalls = smalls + net.swap_dp(smalls, bit)
    step = 1
    while step < mp_size:
        smalls = smalls + net.swap_mp(smalls, step)
        step *= 2

    def own_columns(values):
        return lax.dynamic_slice_in_dim(values, net.mp_at * local_width, local_width, 1)

    return (
        result.reshape(hidden.shape),
        hidden_grad,
        memory_grad,
        self_qkv_grad,
        own_columns(smalls[11:13]),
        self_proj_grad,
        cross_query_grad,
        cross_kv_grad,
        own_columns(smalls[9:11]),
        cross_proj_grad,
        ffn_in_grad.astype(F32),
        lax.dynamic_slice_in_dim(smalls[13:].reshape(-1), net.mp_at * local_ff, local_ff, 0),
        ffn_out_grad.astype(F32),
        smalls[0:3],
        smalls[3:6],
        smalls[6:9],
    )


def solution(mesh):
    dp_size, mp_size = mesh.shape["dp"], mesh.shape["mp"]
    placed = (
        P("dp", None),
        P("dp", "mp"),
        P("dp", None),
        P("dp", None),
        P("dp"),
        P("dp", None),
        P("dp"),
        P(None, None, "mp"),
        P(None, "mp"),
        P("mp", None),
        P(None, "mp"),
        P(None, None, "mp"),
        P(None, "mp"),
        P("mp", None),
        P(None, "mp"),
        P("mp"),
        P("mp", None),
        P(),
        P(),
        P(),
    )

    def local(*arrays):
        return body(dp_size, mp_size, *arrays)

    return jax.shard_map(
        local,
        mesh=mesh,
        in_specs=placed,
        out_specs=(
            P("dp", None),
            P("dp", None),
            P("dp", "mp"),
            P(None, None, "mp"),
            P(None, "mp"),
            P("mp", None),
            P(None, "mp"),
            P(None, None, "mp"),
            P(None, "mp"),
            P("mp", None),
            P(None, "mp"),
            P("mp"),
            P("mp", None),
            P(),
            P(),
            P(),
        ),
        check_vma=False,
    )
```
